32 devices in a mesh: dp: 2 (over y), row: 4 (over z), col: 4 (over x, core).
Axes of the slice: x: 2, y: 2, z: 4, core: 2. Of those that a mesh axis runs over, the one named last changes fastest.
Arguments:
- inputs: bfloat16 [2, 256, 128, 512], P('dp', None, 'row', 'col'), may hold values from -6 to 6
- reduce_weight: bfloat16 [64, 256], replicated, may hold values from -0.375 to 0.375
- spatial_weight: bfloat16 [3, 3, 64, 64], replicated, may hold values from -0.25 to 0.25
- expand_weight: bfloat16 [256, 64], replicated, may hold values from -0.75 to 0.75
- class_weight: bfloat16 [3, 3, 135, 256], replicated, may hold values from -0.125 to 0.125
- anchor_labels: int32 [2, 9, 128, 512], P('dp', None, 'row', 'col'), may hold values from 0 to 15, as said below
- anchor_mask: int32 [2, 9, 128, 512], P('dp', None, 'row', 'col'), may hold values from 0 to 1, as said below
Outputs:
- loss: float32 [], replicated
- grad_reduce: float32 [64, 256], replicated
- grad_spatial: float32 [3, 3, 64, 64], replicated
- grad_expand: float32 [256, 64], replicated
- grad_class: float32 [3, 3, 135, 256], replicated
The draws below stay inside these ranges and needn't reach their ends.
Inputs may be any that keep to these rules, and one draw needn't show every extreme that they name: `anchor_labels`: labels are 0 to 15; anchor 0 at the first row and column of every tile is positive. `anchor_mask`: every anchor with a label above 0 has mask 1.
All inputs are finite; a program needn't handle non-finite values.
Results may differ from the reference program's by a relative error of at most 0.0034.
Values may be sent and summed in bfloat16 or wider, within the bound.
A program may use at most 128 MiB of HBM per device.

```python
import jax
import jax.numpy as jnp
from jax import lax

C = 256
MID = 64
A = 9
K = 15
TILES = 2
H = 128
W = 512


def anchor_pair(key):
    label_key = jax.random.fold_in(key, 11)
    class_key = jax.random.fold_in(key, 12)
    valid_key = jax.random.fold_in(key, 13)
    shape = (TILES, A, H, W)
    tile_index = jnp.arange(TILES, dtype=jnp.int32)[:, None, None, None]
    row_index = jnp.arange(H, dtype=jnp.int32)[None, None, :, None]
    place = tile_index * H + row_index
    threshold = 10 + 20 * place // max(TILES * H - 1, 1)
    rolled = jax.random.randint(label_key, shape, 0, 1000, dtype=jnp.int32)
    classes = jax.random.randint(class_key, shape, 1, K + 1, dtype=jnp.int32)
    labels = jnp.where(rolled < threshold, classes, 0)
    anchor_index = jnp.arange(A, dtype=jnp.int32)[None, :, None, None]
    column_index = jnp.arange(W, dtype=jnp.int32)[None, None, None, :]
    forced = (anchor_index == 0) & (row_index == 0) & (column_index == 0)
    labels = jnp.where(forced, jnp.maximum(classes, 1), labels)
    valid = jax.random.randint(valid_key, shape, 0, 100, dtype=jnp.int32) < 85
    mask = jnp.where((labels > 0) | valid, 1, 0).astype(jnp.int32)
    return (labels.astype(jnp.int32), mask)


def draw_anchor_labels(key, part):
    return anchor_pair(key)[0]


def draw_anchor_mask(key, part):
    return anchor_pair(key)[1]


def levels(key, extent, split, smallest, top_value):
    level = 1.0
    for axis_at, blocks in split:
        steps = jax.random.uniform(jax.random.fold_in(jax.random.fold_in(key, 6), axis_at), (blocks,), jnp.float32, smallest / len(split), top_value / len(split))
        level = level * jnp.repeat(jnp.exp(steps), extent[axis_at] // blocks).reshape((-1,) + (1,) * (len(extent) - 1 - axis_at))
    return level


def scatter_about(key, shape, width, bound, shards=(), kind=jnp.bfloat16):
    entries = width * jax.random.normal(key, shape, jnp.float32)
    if shards:
        entries = entries * levels(key, shape, shards, -0.22, 0.18)
    return jnp.clip(entries, -bound, bound).astype(kind)


def setup_inputs(seed: int = 0) -> dict:
    arg_keys = jax.random.split(jax.random.key(seed), 8)
    inputs = scatter_about(arg_keys[0], (TILES, C, H, W), 1.0, 6.0, ((0, 2), (2, 4), (3, 4)))
    reduce_weight = scatter_about(arg_keys[1], (MID, C), C ** -0.5, 0.375)
    spatial_weight = scatter_about(arg_keys[2], (3, 3, MID, MID), (9 * MID) ** -0.5, 0.25)
    expand_weight = scatter_about(arg_keys[3], (C, MID), MID ** -0.5, 0.75)
    class_weight = scatter_about(arg_keys[4], (3, 3, A * K, C), (9 * C) ** -0.5, 0.125)
    anchor_labels = draw_anchor_labels(jax.random.fold_in(arg_keys[7], 71), 0)
    anchor_mask = draw_anchor_mask(jax.random.fold_in(arg_keys[7], 71), 0)
    return dict(inputs=inputs, reduce_weight=reduce_weight, spatial_weight=spatial_weight, expand_weight=expand_weight, class_weight=class_weight, anchor_labels=anchor_labels, anchor_mask=anchor_mask)


def conv_three(padded, weight, rows, cols):
    total = jnp.zeros((padded.shape[0], weight.shape[2], rows, cols), jnp.float32)
    for dy in range(3):
        for dx in range(3):
            total = total + jnp.einsum('oc,bchw->bohw', weight[dy, dx].astype(jnp.float32), padded[:, :, dy:dy + rows, dx:dx + cols].astype(jnp.float32), precision=lax.Precision.HIGHEST)
    return total

def weight_three(dout, padded, rows, cols):
    taps = []
    for dy in range(3):
        for dx in range(3):
            taps.append(jnp.einsum('bohw,bchw->oc', dout.astype(jnp.float32), padded[:, :, dy:dy + rows, dx:dx + cols].astype(jnp.float32), precision=lax.Precision.HIGHEST))
    return jnp.stack(taps).reshape(3, 3, taps[0].shape[0], taps[0].shape[1])

def input_three(dout_pad, weight, rows, cols):
    total = jnp.zeros((dout_pad.shape[0], weight.shape[3], rows, cols), jnp.float32)
    for ey in range(3):
        for ex in range(3):
            total = total + jnp.einsum('oc,bohw->bchw', weight[2 - ey, 2 - ex].astype(jnp.float32), dout_pad[:, :, ey:ey + rows, ex:ex + cols].astype(jnp.float32), precision=lax.Precision.HIGHEST)
    return total

def focal_terms(logits, labels, mask):
    shaped = logits.reshape(logits.shape[0], A, K, logits.shape[2], logits.shape[3])
    classes = jnp.arange(1, K + 1, dtype=jnp.int32)[None, None, :, None, None]
    target = labels[:, :, None] == classes
    signs = jnp.where(target, 1.0, -1.0).astype(shaped.dtype)
    alpha = jnp.where(target, 0.25, 0.75).astype(shaped.dtype)
    terms = -alpha * jax.nn.sigmoid(-signs * shaped) ** 2 * jax.nn.log_sigmoid(signs * shaped)
    return jnp.sum(terms * mask[:, :, None].astype(shaped.dtype))

def pad_cells(field):
    return jnp.pad(field, ((0, 0), (0, 0), (1, 1), (1, 1)))

def one_tile(inputs, labels, mask, reduce_weight, spatial_weight, expand_weight, class_weight):
    rows, cols = (inputs.shape[2], inputs.shape[3])
    first = jax.nn.relu(jnp.einsum('mc,bchw->bmhw', reduce_weight.astype(jnp.float32), inputs.astype(jnp.float32), precision=lax.Precision.HIGHEST)).astype(jnp.bfloat16)
    first_pad = pad_cells(first)
    second = jax.nn.relu(conv_three(first_pad, spatial_weight, rows, cols)).astype(jnp.bfloat16)
    block = jax.nn.relu(inputs.astype(jnp.float32) + jnp.einsum('cm,bmhw->bchw', expand_weight.astype(jnp.float32), second.astype(jnp.float32), precision=lax.Precision.HIGHEST)).astype(jnp.bfloat16)
    block_pad = pad_cells(block)
    logits = conv_three(block_pad, class_weight, rows, cols)
    focal, pullback = jax.vjp(lambda z: focal_terms(z, labels, mask), logits)
    dlogits = pullback(jnp.ones_like(focal))[0].astype(jnp.bfloat16)
    count = jnp.sum((labels > 0).astype(jnp.float32))
    class_sum = weight_three(dlogits, block_pad, rows, cols)
    dblock = input_three(pad_cells(dlogits), class_weight, rows, cols)
    dsum = jnp.where(block > 0, dblock, 0.0).astype(jnp.bfloat16)
    expand_sum = jnp.einsum('bchw,bmhw->cm', dsum.astype(jnp.float32), second.astype(jnp.float32), precision=lax.Precision.HIGHEST)
    dsecond = jnp.where(second > 0, jnp.einsum('cm,bchw->bmhw', expand_weight.astype(jnp.float32), dsum.astype(jnp.float32), precision=lax.Precision.HIGHEST), 0.0).astype(jnp.bfloat16)
    spatial_sum = weight_three(dsecond, first_pad, rows, cols)
    dfirst = jnp.where(first > 0, input_three(pad_cells(dsecond), spatial_weight, rows, cols), 0.0).astype(jnp.bfloat16)
    reduce_sum = jnp.einsum('bmhw,bchw->mc', dfirst.astype(jnp.float32), inputs.astype(jnp.float32), precision=lax.Precision.HIGHEST)
    return (reduce_sum, spatial_sum, expand_sum, class_sum, focal, count)

def reference(inputs, reduce_weight, spatial_weight, expand_weight, class_weight, anchor_labels, anchor_mask):

    def per_tile(items):
        return one_tile(items[0][None], items[1][None], items[2][None], reduce_weight, spatial_weight, expand_weight, class_weight)
    results = lax.map(per_tile, (inputs, anchor_labels, anchor_mask))
    summed = [lax.optimization_barrier(jnp.sum(item, axis=0)) for item in results]
    positives = summed[5]
    loss = summed[4] / positives
    return (loss, summed[0] / positives, summed[1] / positives, summed[2] / positives, summed[3] / positives)
```

```python
import functools

import jax
import jax.numpy as jnp
import numpy as np
from jax import lax
from jax.experimental import pallas as pl
from jax.experimental.pallas import tpu as pltpu
from jax.sharding import PartitionSpec as P

A = 9
K = 15
HALO = 4
STEP = 512
EDGE = 256
F32 = jnp.float32
BF16 = jnp.bfloat16
AXES = ("dp", "row", "col")


def extended(cells, sides, width):
    for axis, dim in sides:
        count = lax.axis_size(axis)
        ends = count - 1
        head = lax.slice_in_dim(cells, 0, width, axis=dim)
        tail = lax.slice_in_dim(cells, cells.shape[dim] - width, cells.shape[dim], axis=dim)
        cells = jnp.concatenate(
            [
                lax.ppermute(tail, axis, [(i, (i + 1) % count) for i in range(ends)]),
                cells,
                lax.ppermute(head, axis, [((i + 1) % count, i) for i in range(ends)]),
            ],
            axis=dim,
        )
    return cells


def dot(a, b):
    return jnp.dot(a, b, preferred_element_type=F32)


def dot_t(a, b):
    return lax.dot_general(a, b, (((1,), (1,)), ((), ())), preferred_element_type=F32)


def tile_kernel(
    pitch, geo,
    x_ref, own_ref, spread_ref, wr_ref, ws_ref, wsb_ref, we_ref, wet_ref, wc_ref, wcb_ref,
    reduce_ref, spatial_ref, expand_ref, class_ref, focal_ref, count_ref,
    first, second, block, dlog, dsec, big, small, acc_c,
):
    chans = we_ref.shape[0]
    mid = we_ref.shape[1]
    outs = wc_ref.shape[0]
    length = x_ref.shape[1]
    shifts = [(dy - 1) * pitch + (dx - 1) for dy in range(3) for dx in range(3)]

    def columns(ref, base, sign, dest):
        rows = ref.shape[0]
        window = ref[:, pl.ds(base, STEP + 2 * EDGE)]
        for tap, shift in enumerate(shifts):
            at = EDGE + sign * shift
            dest[tap * rows:(tap + 1) * rows, :] = window[:, at:at + STEP]

    def at(i, start):
        return pl.multiple_of(start + i * STEP, 128)

    def loop(start, steps, body, init=0):
        return lax.fori_loop(0, steps, lambda i, c: body(at(i, start), c), init)

    first[:, :EDGE] = jnp.zeros((mid, EDGE), BF16)
    first[:, EDGE + length:] = jnp.zeros((mid, EDGE), BF16)
    dlog[...] = jnp.zeros_like(dlog)
    acc_c[...] = jnp.zeros_like(acc_c)
    reduce_ref[...] = jnp.zeros_like(reduce_ref)
    spatial_ref[...] = jnp.zeros_like(spatial_ref)
    expand_ref[...] = jnp.zeros_like(expand_ref)

    def make_first(p, c):
        z = dot(wr_ref[...], x_ref[:chans, pl.ds(p, STEP)])
        first[:, pl.ds(pl.multiple_of(p + EDGE, 128), STEP)] = jnp.maximum(z, 0.0).astype(BF16)
        return c

    loop(0, length // STEP, make_first)

    def make_block(p, c):
        columns(first, p, 1, small)
        s = jnp.maximum(dot(ws_ref[...], small[...]), 0.0).astype(BF16)
        second[:, pl.ds(p, STEP)] = s
        xs = x_ref[:, pl.ds(p, STEP)]
        valid = xs[chans + A:chans + A + 1].astype(F32)
        b = jnp.maximum(xs[:chans].astype(F32) + dot(we_ref[...], s), 0.0) * valid
        block[:, pl.ds(p, STEP)] = b.astype(BF16)
        return c

    loop(0, length // STEP, make_block)

    ident = lax.rem(lax.broadcasted_iota(jnp.int32, (outs, 1), 0), K) + 1

    def make_dlog(p, carry):
        total, count = carry
        columns(block, pl.multiple_of(p - EDGE, 128), 1, big)
        z = dot(wc_ref[...], big[...])
        code = x_ref[chans:, pl.ds(p, STEP)]
        own = own_ref[:, pl.ds(p, STEP)]
        wide = dot(spread_ref[...], code)
        live = wide >= 15.5
        label = jnp.where(live, wide - 16.0, wide)
        target = label == ident.astype(F32)
        alpha = jnp.where(target, 0.25, 0.75)
        alpha = jnp.where(live, alpha, 0.0)
        u = jnp.where(target, -z, z)
        e = jnp.exp(-jnp.abs(u))
        inv = 1.0 / (1.0 + e)
        low = e * inv
        pos = u >= 0.0
        prob = jnp.where(pos, inv, low)
        rest = jnp.where(pos, low, inv)
        soft = jnp.maximum(u, 0.0) + jnp.log1p(e)
        scaled = alpha * prob * prob
        total = total + jnp.sum(scaled * soft, axis=0, keepdims=True) * own
        slope = scaled * (2.0 * rest * soft + prob)
        d = jnp.where(target, -slope, slope).astype(BF16)
        dlog[:, pl.ds(p, STEP)] = d
        mine = (d.astype(F32) * own).astype(BF16)
        acc_c[...] += dot_t(mine, big[...])
        codes = code.astype(F32)
        labels = jnp.where(codes >= 15.5, codes - 16.0, codes)
        row = lax.broadcasted_iota(jnp.int32, codes.shape, 0)
        hit = jnp.where((labels > 0.5) & (row < A), 1.0, 0.0)
        count = count + jnp.sum(hit, axis=0, keepdims=True) * own
        return total, count

    zero = jnp.zeros((1, STEP), F32)
    total, count = loop(geo[0][0], geo[0][1], make_dlog, (zero, zero))
    focal_ref[...] = jnp.sum(total, keepdims=True).reshape(1, 1)
    count_ref[...] = jnp.sum(count, keepdims=True).reshape(1, 1)

    def make_dsec(p, c):
        columns(dlog, pl.multiple_of(p - EDGE, 128), -1, big.at[:9 * outs])
        g = dot(wcb_ref[...], big[:9 * outs, :])
        b = block[:, pl.ds(p, STEP)].astype(F32)
        ds = jnp.where(b > 0.0, g, 0.0).astype(BF16)
        s = second[:, pl.ds(p, STEP)]
        own = own_ref[:, pl.ds(p, STEP)]
        sf = s.astype(F32)
        expand_ref[...] += dot_t(ds, (sf * own).astype(BF16))
        h = dot(wet_ref[...], ds)
        dsec[:, pl.ds(p, STEP)] = jnp.where(sf > 0.0, h, 0.0).astype(BF16)
        return c

    loop(geo[0][0], geo[0][1], make_dsec)

    def make_dfirst(p, c):
        own = own_ref[:, pl.ds(p, STEP)]
        columns(first, p, 1, small)
        mine = (dsec[:, pl.ds(p, STEP)].astype(F32) * own).astype(BF16)
        spatial_ref[...] += dot_t(mine, small[...])
        columns(dsec, pl.multiple_of(p - EDGE, 128), -1, small)
        g = dot(wsb_ref[...], small[...]) * own
        f = first[:, pl.ds(pl.multiple_of(p + EDGE, 128), STEP)].astype(F32)
        df = jnp.where(f > 0.0, g, 0.0).astype(BF16)
        reduce_ref[...] += dot_t(df, x_ref[:chans, pl.ds(p, STEP)])
        return c

    loop(geo[1][0], geo[1][1], make_dfirst)
    for tap in range(9):
        class_ref[tap] = acc_c[:, tap * chans:(tap + 1) * chans]


def per_device(
    inputs, reduce_weight, spatial_weight, expand_weight, class_weight, anchor_labels, anchor_mask
):
    tiles, chans, rows, cols = inputs.shape
    mid = reduce_weight.shape[0]
    heads = class_weight.shape[2]
    outs = -(-heads // 16) * 16
    tall, pitch = rows + 2 * HALO, cols + 2 * HALO
    pixels = tall * pitch
    length = -(-pixels // STEP) * STEP

    def span(margin):
        low = margin * pitch + margin
        high = (tall - margin) * pitch
        start = max(EDGE, low // 128 * 128 // EDGE * EDGE)
        return start, -(-(high - start) // STEP)

    geo = (span(2), span(4))
    need = geo[0][0] + geo[0][1] * STEP + EDGE
    length = max(length, -(-need // STEP) * STEP)

    code = (anchor_labels + 16 * anchor_mask).astype(BF16)
    ones = jnp.ones((tiles, 1, rows, cols), BF16)
    none = jnp.zeros((tiles, 16 - A - 1, rows, cols), BF16)
    field = jnp.concatenate([inputs, code, ones, none], axis=1)
    field = extended(field, (("row", 2), ("col", 3)), HALO)
    field = field.reshape(tiles, chans + 16, pixels)
    field = jnp.pad(field, ((0, 0), (0, 0), (0, length - pixels)))

    own = np.zeros((tall, pitch), np.float32)
    own[HALO:HALO + rows, HALO:HALO + cols] = 1.0
    own = jnp.asarray(np.pad(own.reshape(1, pixels), ((0, 0), (0, length - pixels))))
    spread = np.zeros((outs, 16), np.float32)
    spread[np.arange(heads), np.arange(heads) // K] = 1.0
    spread = jnp.asarray(spread, BF16)

    ws = spatial_weight.transpose(2, 0, 1, 3).reshape(mid, 9 * mid)
    wsb = spatial_weight.transpose(3, 0, 1, 2).reshape(mid, 9 * mid)
    wide = jnp.pad(class_weight, ((0, 0), (0, 0), (0, outs - heads), (0, 0)))
    wc = wide.transpose(2, 0, 1, 3).reshape(outs, 9 * chans)
    wcb = wide.transpose(3, 0, 1, 2).reshape(chans, 9 * outs)

    call = pl.pallas_call(
        functools.partial(tile_kernel, pitch, geo),
        out_shape=(
            jax.ShapeDtypeStruct((mid, chans), F32),
            jax.ShapeDtypeStruct((mid, 9 * mid), F32),
            jax.ShapeDtypeStruct((chans, mid), F32),
            jax.ShapeDtypeStruct((9, outs, chans), F32),
            jax.ShapeDtypeStruct((1, 1), F32),
            jax.ShapeDtypeStruct((1, 1), F32),
        ),
        in_specs=[pl.BlockSpec(memory_space=pltpu.VMEM)] * 10,
        out_specs=[pl.BlockSpec(memory_space=pltpu.VMEM)] * 6,
        scratch_shapes=[
            pltpu.VMEM((mid, length + 2 * EDGE), BF16),
            pltpu.VMEM((mid, length), BF16),
            pltpu.VMEM((chans, length), BF16),
            pltpu.VMEM((outs, length), BF16),
            pltpu.VMEM((mid, length), BF16),
            pltpu.VMEM((9 * chans, STEP), BF16),
            pltpu.VMEM((9 * mid, STEP), BF16),
            pltpu.VMEM((outs, 9 * chans), F32),
        ],
        compiler_params=pltpu.CompilerParams(vmem_limit_bytes=50 * 1024 * 1024),
        name="tile_step",
    )
    sums = None
    for t in range(tiles):
        part = call(
            field[t], own, spread, reduce_weight, ws, wsb, expand_weight, expand_weight.T, wc, wcb
        )
        sums = part if sums is None else tuple(a + b for a, b in zip(sums, part))
    return finish(sums, mid, heads)


def finish(sums, mid, heads):
    reduce_sum, spatial_sum, expand_sum, class_sum, focal, count = lax.psum(sums, AXES)
    chans = reduce_sum.shape[1]
    count = count[0, 0]
    scale = 1.0 / count
    spatial = spatial_sum.reshape(mid, 3, 3, mid).transpose(1, 2, 0, 3)
    return (
        focal[0, 0] / count,
        reduce_sum * scale,
        spatial * scale,
        expand_sum * scale,
        class_sum[:, :heads].reshape(3, 3, heads, chans) * scale,
    )


def solution(mesh):
    tiled = P("dp", None, "row", "col")
    return jax.shard_map(
        per_device,
        mesh=mesh,
        in_specs=(tiled, P(), P(), P(), P(), tiled, tiled),
        out_specs=(P(), P(), P(), P(), P()),
        check_vma=False,
    )
```

```python
import functools

import jax
import jax.numpy as jnp
import numpy as np
from jax import lax
from jax.experimental import pallas as pl
from jax.experimental.pallas import tpu as pltpu
from jax.sharding import PartitionSpec as P

A = 9
K = 15
HALO = 4
STEP = 512
EDGE = 256
F32 = jnp.float32
BF16 = jnp.bfloat16
AXES = ("dp", "row", "col")


def extended(cells, sides, width):
    for axis, dim in sides:
        count = lax.axis_size(axis)
        ends = count - 1
        head = lax.slice_in_dim(cells, 0, width, axis=dim)
        tail = lax.slice_in_dim(cells, cells.shape[dim] - width, cells.shape[dim], axis=dim)
        cells = jnp.concatenate(
            [
                lax.ppermute(tail, axis, [(i, (i + 1) % count) for i in range(ends)]),
                cells,
                lax.ppermute(head, axis, [((i + 1) % count, i) for i in range(ends)]),
            ],
            axis=dim,
        )
    return cells


def dot(a, b):
    return jnp.dot(a, b, preferred_element_type=F32)


def dot_t(a, b):
    return lax.dot_general(a, b, (((1,), (1,)), ((), ())), preferred_element_type=F32)


def tile_kernel(
    pitch, geo, heads_in,
    mid_ref, left_ref, right_ref, own_ref, spread_ref, wr_ref, ws_ref, wsb_ref, we_ref, wet_ref, wc_ref, wcb_ref,
    pack_ref, stat_ref,
    x_ref, first, second, block, dlog, dsec, big, small, acc_c, reduce_ref, spatial_ref, expand_ref,
):
    chans = we_ref.shape[0]
    mid = we_ref.shape[1]
    outs = wc_ref.shape[0]
    length = x_ref.shape[1]
    shifts = [(dy - 1) * pitch + (dx - 1) for dy in range(3) for dx in range(3)]

    def columns(ref, base, sign, dest):
        rows = ref.shape[0]
        window = ref[:, pl.ds(base, STEP + 2 * EDGE)]
        for tap, shift in enumerate(shifts):
            at = EDGE + sign * shift
            dest[tap * rows:(tap + 1) * rows, :] = window[:, at:at + STEP]

    def at(i, start):
        return pl.multiple_of(start + i * STEP, 128)

    def loop(start, steps, body, init=0):
        return lax.fori_loop(0, steps, lambda i, c: body(at(i, start), c), init)

    tall, _, cols = mid_ref.shape
    x_ref[:, tall * pitch // 128 * 128:] = jnp.zeros(
        (x_ref.shape[0], length - tall * pitch // 128 * 128), BF16
    )
    for h in range(tall):
        x_ref[:, h * pitch:h * pitch + HALO] = left_ref[h]
        x_ref[:, h * pitch + HALO:h * pitch + HALO + cols] = mid_ref[h]
        x_ref[:, h * pitch + HALO + cols:(h + 1) * pitch] = right_ref[h]

    first[:, :EDGE] = jnp.zeros((mid, EDGE), BF16)
    first[:, EDGE + length:] = jnp.zeros((mid, EDGE), BF16)
    dlog[...] = jnp.zeros_like(dlog)
    acc_c[...] = jnp.zeros_like(acc_c)
    reduce_ref[...] = jnp.zeros_like(reduce_ref)
    spatial_ref[...] = jnp.zeros_like(spatial_ref)
    expand_ref[...] = jnp.zeros_like(expand_ref)

    def make_first(p, c):
        z = dot(wr_ref[...], x_ref[:chans, pl.ds(p, STEP)])
        first[:, pl.ds(pl.multiple_of(p + EDGE, 128), STEP)] = jnp.maximum(z, 0.0).astype(BF16)
        return c

    loop(0, length // STEP, make_first)

    def make_block(p, c):
        columns(first, p, 1, small)
        s = jnp.maximum(dot(ws_ref[...], small[...]), 0.0).astype(BF16)
        second[:, pl.ds(p, STEP)] = s
        xs = x_ref[:, pl.ds(p, STEP)]
        valid = xs[chans + A:chans + A + 1].astype(F32)
        b = jnp.maximum(xs[:chans].astype(F32) + dot(we_ref[...], s), 0.0) * valid
        block[:, pl.ds(p, STEP)] = b.astype(BF16)
        return c

    loop(0, length // STEP, make_block)

    ident = lax.rem(lax.broadcasted_iota(jnp.int32, (outs, 1), 0), K) + 1

    def make_dlog(p, carry):
        total, count = carry
        columns(block, pl.multiple_of(p - EDGE, 128), 1, big)
        z = dot(wc_ref[...], big[...])
        code = x_ref[chans:, pl.ds(p, STEP)]
        own = own_ref[:, pl.ds(p, STEP)]
        wide = dot(spread_ref[...], code)
        live = wide >= 15.5
        label = jnp.where(live, wide - 16.0, wide)
        target = label == ident.astype(F32)
        alpha = jnp.where(target, 0.25, 0.75)
        alpha = jnp.where(live, alpha, 0.0)
        u = jnp.where(target, -z, z)
        e = jnp.exp(-jnp.abs(u))
        inv = 1.0 / (1.0 + e)
        low = e * inv
        pos = u >= 0.0
        prob = jnp.where(pos, inv, low)
        rest = jnp.where(pos, low, inv)
        soft = jnp.maximum(u, 0.0) + jnp.log1p(e)
        scaled = alpha * prob * prob
        total = total + jnp.sum(scaled * soft, axis=0, keepdims=True) * own
        slope = scaled * (2.0 * rest * soft + prob)
        d = jnp.where(target, -slope, slope).astype(BF16)
        dlog[:, pl.ds(p, STEP)] = d
        mine = (d.astype(F32) * own).astype(BF16)
        acc_c[...] += dot_t(mine, big[...])
        codes = code.astype(F32)
        labels = jnp.where(codes >= 15.5, codes - 16.0, codes)
        row = lax.broadcasted_iota(jnp.int32, codes.shape, 0)
        hit = jnp.where((labels > 0.5) & (row < A), 1.0, 0.0)
        count = count + jnp.sum(hit, axis=0, keepdims=True) * own
        return total, count

    zero = jnp.zeros((1, STEP), F32)
    total, count = loop(geo[0][0], geo[0][1], make_dlog, (zero, zero))
    stat_ref[0:1, :] = sum(total[:, k * 128:(k + 1) * 128] for k in range(STEP // 128))
    stat_ref[1:2, :] = sum(count[:, k * 128:(k + 1) * 128] for k in range(STEP // 128))
    stat_ref[2:, :] = jnp.zeros((6, 128), F32)

    def make_dsec(p, c):
        columns(dlog, pl.multiple_of(p - EDGE, 128), -1, big.at[:9 * outs])
        g = dot(wcb_ref[...], big[:9 * outs, :])
        b = block[:, pl.ds(p, STEP)].astype(F32)
        ds = jnp.where(b > 0.0, g, 0.0).astype(BF16)
        s = second[:, pl.ds(p, STEP)]
        own = own_ref[:, pl.ds(p, STEP)]
        sf = s.astype(F32)
        expand_ref[...] += dot_t((sf * own).astype(BF16), ds)
        h = dot(wet_ref[...], ds)
        dsec[:, pl.ds(p, STEP)] = jnp.where(sf > 0.0, h, 0.0).astype(BF16)
        return c

    loop(geo[0][0], geo[0][1], make_dsec)

    def make_dfirst(p, c):
        own = own_ref[:, pl.ds(p, STEP)]
        columns(first, p, 1, small)
        mine = (dsec[:, pl.ds(p, STEP)].astype(F32) * own).astype(BF16)
        spatial_ref[...] += dot_t(mine, small[...])
        columns(dsec, pl.multiple_of(p - EDGE, 128), -1, small)
        g = dot(wsb_ref[...], small[...]) * own
        f = first[:, pl.ds(pl.multiple_of(p + EDGE, 128), STEP)].astype(F32)
        df = jnp.where(f > 0.0, g, 0.0).astype(BF16)
        reduce_ref[...] += dot_t(df, x_ref[:chans, pl.ds(p, STEP)])
        return c

    loop(geo[1][0], geo[1][1], make_dfirst)
    heads = heads_in
    spots = layout(mid, heads)[:3]
    pack_ref[...] = jnp.zeros_like(pack_ref)
    for tap in range(9):
        pack_ref[tap * heads:(tap + 1) * heads, :] = acc_c[:heads, tap * chans:(tap + 1) * chans]
    pack_ref[spots[0]:spots[0] + mid, :] = reduce_ref[...]
    pack_ref[spots[1]:spots[1] + mid, :] = expand_ref[...]
    for dy in range(3):
        at_row = spots[2] + dy * mid
        pack_ref[at_row:at_row + mid, :3 * mid] = spatial_ref[:, dy * 3 * mid:(dy + 1) * 3 * mid]


def layout(mid, heads):
    first = -(-9 * heads // 8) * 8
    return first, first + mid, first + 2 * mid, first + 5 * mid


def piece_rows(s, orders, sizes, total):
    rows, out = total // len(orders), []
    for axis in orders[s]:
        rows //= sizes[axis]
        out.append(rows)
    return out


def sum_kernel(sizes, orders, pack_ref, stat_ref, out_ref, total_ref, *scratch):
    subs, depth = len(orders), len(AXES)
    send, full = scratch[0], scratch[1]
    recvs = [scratch[2 + s * depth:2 + (s + 1) * depth] for s in range(subs)]
    stat_send = scratch[2 + subs * depth]
    stat_recv = scratch[3 + subs * depth:3 + subs * depth + depth]
    ssem, rsem = scratch[-2:]
    total = pack_ref.shape[0]
    share = total // subs
    me = {axis: lax.axis_index(axis) for axis in AXES}
    peers = lambda axis: range(1, sizes[axis])
    mesh_id = pl.DeviceIdType.MESH

    barrier = pltpu.get_barrier_semaphore()
    for axis in AXES:
        for d in peers(axis):
            pl.semaphore_signal(
                barrier, inc=1, device_id={axis: lax.rem(me[axis] + d, sizes[axis])},
                device_id_type=mesh_id,
            )
    pl.semaphore_wait(barrier, sum(sizes[axis] - 1 for axis in AXES))

    used = [0]

    def push(src, dst, axis, d):
        n = used[0]
        used[0] += 1
        copy = pltpu.make_async_remote_copy(
            src_ref=src, dst_ref=dst, send_sem=ssem.at[n], recv_sem=rsem.at[n],
            device_id={axis: lax.rem(me[axis] + d, sizes[axis])}, device_id_type=mesh_id,
        )
        copy.start()
        return copy

    send[...] = pack_ref[...].astype(BF16)
    base = [s * share for s in range(subs)]
    held = [None] * subs
    stat = stat_ref[...]
    for k in range(depth):
        copies = []
        for s in range(subs):
            axis = orders[s][k]
            rows = piece_rows(s, orders, sizes, total)[k]
            for d in peers(axis):
                to = lax.rem(me[axis] + d, sizes[axis])
                src = send.at[pl.ds(pl.multiple_of(base[s] + to * rows, 16), rows)]
                copies.append(push(src, recvs[s][k].at[d - 1], axis, d))
        stat_send[k] = stat
        for d in peers(AXES[k]):
            copies.append(push(stat_send.at[k], stat_recv[k].at[d - 1], AXES[k], d))
        for copy in copies:
            copy.wait()
        for d in peers(AXES[k]):
            stat = stat + stat_recv[k][d - 1]
        for s in range(subs):
            axis = orders[s][k]
            rows = piece_rows(s, orders, sizes, total)[k]
            mine = me[axis] * rows
            if k == 0:
                got = pack_ref[pl.ds(pl.multiple_of(base[s] + mine, 16), rows), :]
            else:
                out_at = pl.ds(pl.multiple_of(base[s] + mine, 16), rows)
                got = out_ref[out_at, :]
            for d in peers(axis):
                got = got + recvs[s][k][d - 1].astype(F32)
            base[s] = pl.multiple_of(base[s] + mine, 16)
            where = pl.ds(base[s], rows)
            if k < depth - 1:
                out_ref[where, :] = got
                send[where, :] = got.astype(BF16)
            else:
                full[where, :] = got.astype(BF16)
    total_ref[...] = stat
    for k in range(depth - 1, -1, -1):
        copies = []
        for s in range(subs):
            axis = orders[s][k]
            rows = piece_rows(s, orders, sizes, total)[k]
            where = pl.ds(base[s], rows)
            for d in peers(axis):
                copies.append(push(full.at[where], full.at[where], axis, d))
            base[s] = pl.multiple_of(base[s] - me[axis] * rows, 16)
        for copy in copies:
            copy.wait()
    out_ref[...] = full[...].astype(F32)


def sum_devices(pack, stat):
    sizes = {axis: lax.axis_size(axis) for axis in AXES}
    orders = [AXES[s:] + AXES[:s] for s in range(len(AXES))]
    total, chans = pack.shape
    scratch = [pltpu.VMEM((total, chans), BF16), pltpu.VMEM((total, chans), BF16)]
    copies = 0
    for s in range(len(orders)):
        for axis, rows in zip(orders[s], piece_rows(s, orders, sizes, total)):
            scratch.append(pltpu.VMEM((max(sizes[axis] - 1, 1), rows, chans), BF16))
            copies += 2 * (sizes[axis] - 1)
    scratch.append(pltpu.VMEM((len(AXES),) + stat.shape, F32))
    for axis in AXES:
        scratch.append(pltpu.VMEM((max(sizes[axis] - 1, 1),) + stat.shape, F32))
        copies += sizes[axis] - 1
    scratch += [pltpu.SemaphoreType.DMA((copies,)), pltpu.SemaphoreType.DMA((copies,))]
    return pl.pallas_call(
        functools.partial(sum_kernel, sizes, orders),
        out_shape=(
            jax.ShapeDtypeStruct(pack.shape, F32), jax.ShapeDtypeStruct(stat.shape, F32)
        ),
        in_specs=[pl.BlockSpec(memory_space=pltpu.VMEM)] * 2,
        out_specs=[pl.BlockSpec(memory_space=pltpu.VMEM)] * 2,
        scratch_shapes=scratch,
        compiler_params=pltpu.CompilerParams(
            collective_id=0, has_side_effects=True, vmem_limit_bytes=16 * 1024 * 1024
        ),
        name="sum_devices",
    )(pack, stat)


def per_device(
    inputs, reduce_weight, spatial_weight, expand_weight, class_weight, anchor_labels, anchor_mask
):
    tiles, chans, rows, cols = inputs.shape
    mid = reduce_weight.shape[0]
    heads = class_weight.shape[2]
    outs = -(-heads // 16) * 16
    tall, pitch = rows + 2 * HALO, cols + 2 * HALO
    pixels = tall * pitch
    length = -(-pixels // STEP) * STEP

    def span(margin):
        low = margin * pitch + margin
        high = (tall - margin) * pitch
        start = max(EDGE, low // 128 * 128 // EDGE * EDGE)
        return start, -(-(high - start) // STEP)

    geo = (span(2), span(4))
    need = geo[0][0] + geo[0][1] * STEP + EDGE
    length = max(length, -(-need // STEP) * STEP)

    code = (anchor_labels + 16 * anchor_mask).astype(BF16)
    ones = jnp.ones((tiles, 1, rows, cols), BF16)
    none = jnp.zeros((tiles, 16 - A - 1, rows, cols), BF16)
    field = jnp.concatenate([inputs, code, ones, none], axis=1)
    field = extended(field, (("row", 2),), HALO)
    ends = lax.axis_size("col") - 1
    left = lax.ppermute(field[..., -HALO:], "col", [(i, i + 1) for i in range(ends)])
    right = lax.ppermute(field[..., :HALO], "col", [(i + 1, i) for i in range(ends)])
    field, left, right = (v.transpose(0, 2, 1, 3) for v in (field, left, right))

    own = np.zeros((tall, pitch), np.float32)
    own[HALO:HALO + rows, HALO:HALO + cols] = 1.0
    own = jnp.asarray(np.pad(own.reshape(1, pixels), ((0, 0), (0, length - pixels))))
    spread = np.zeros((outs, 16), np.float32)
    spread[np.arange(heads), np.arange(heads) // K] = 1.0
    spread = jnp.asarray(spread, BF16)

    ws = spatial_weight.transpose(2, 0, 1, 3).reshape(mid, 9 * mid)
    wsb = spatial_weight.transpose(3, 0, 1, 2).reshape(mid, 9 * mid)
    wide = jnp.pad(class_weight, ((0, 0), (0, 0), (0, outs - heads), (0, 0)))
    wc = wide.transpose(2, 0, 1, 3).reshape(outs, 9 * chans)
    wcb = wide.transpose(3, 0, 1, 2).reshape(chans, 9 * outs)

    unit = 16 * len(AXES) * int(np.prod([lax.axis_size(axis) for axis in AXES]))
    packed = -(-layout(mid, heads)[3] // unit) * unit

    call = pl.pallas_call(
        functools.partial(tile_kernel, pitch, geo, heads),
        out_shape=(
            jax.ShapeDtypeStruct((packed, chans), F32),
            jax.ShapeDtypeStruct((8, 128), F32),
        ),
        in_specs=[pl.BlockSpec(memory_space=pltpu.VMEM)] * 12,
        out_specs=[pl.BlockSpec(memory_space=pltpu.VMEM)] * 2,
        scratch_shapes=[
            pltpu.VMEM((chans + 16, length), BF16),
            pltpu.VMEM((mid, length + 2 * EDGE), BF16),
            pltpu.VMEM((mid, length), BF16),
            pltpu.VMEM((chans, length), BF16),
            pltpu.VMEM((outs, length), BF16),
            pltpu.VMEM((mid, length), BF16),
            pltpu.VMEM((9 * chans, STEP), BF16),
            pltpu.VMEM((9 * mid, STEP), BF16),
            pltpu.VMEM((outs, 9 * chans), F32),
            pltpu.VMEM((mid, chans), F32),
            pltpu.VMEM((mid, 9 * mid), F32),
            pltpu.VMEM((mid, chans), F32),
        ],
        compiler_params=pltpu.CompilerParams(vmem_limit_bytes=50 * 1024 * 1024),
        name="tile_step",
    )
    sums = None
    for t in range(tiles):
        part = call(
            field[t], left[t], right[t], own, spread, reduce_weight, ws, wsb, expand_weight, expand_weight.T, wc, wcb
        )
        sums = part if sums is None else tuple(a + b for a, b in zip(sums, part))
    return finish(sums, mid, heads)


def finish(sums, mid, heads):
    pack, stat = sum_devices(*sums)
    chans = pack.shape[1]
    spots = layout(mid, heads)
    count = jnp.sum(stat[1])
    scale = 1.0 / count
    spatial = pack[spots[2]:spots[3], :3 * mid].reshape(3, mid, 3, mid).transpose(0, 2, 1, 3)
    return (
        jnp.sum(stat[0]) / count,
        pack[spots[0]:spots[1]] * scale,
        spatial * scale,
        pack[spots[1]:spots[2]].T * scale,
        pack[:9 * heads].reshape(3, 3, heads, chans) * scale,
    )


def solution(mesh):
    tiled = P("dp", None, "row", "col")
    return jax.shard_map(
        per_device,
        mesh=mesh,
        in_specs=(tiled, P(), P(), P(), P(), tiled, tiled),
        out_specs=(P(), P(), P(), P(), P()),
        check_vma=False,
    )
```

```python
import functools

import jax
import jax.numpy as jnp
import numpy as np
from jax import lax
from jax.experimental import pallas as pl
from jax.experimental.pallas import tpu as pltpu
from jax.sharding import PartitionSpec as P

A = 9
K = 15
HALO = 4
STEP = 512
EDGE = 256
F32 = jnp.float32
BF16 = jnp.bfloat16
AXES = ("dp", "row", "col")


def row_of(mid_ref, top_ref, low_ref, h):
    rows = mid_ref.shape[0]
    if h < HALO:
        return top_ref[h]
    if h < HALO + rows:
        return mid_ref[h - HALO]
    return low_ref[h - HALO - rows]


def halo_kernel(
    sizes, mid_ref, top_ref, low_ref, left_ref, right_ref,
    got_top, got_low, send_left, send_right, got_left, got_right, ssem, rsem,
):
    rows, _, cols = mid_ref.shape
    tall = rows + 2 * HALO
    me = {axis: lax.axis_index(axis) for axis in ("row", "col")}
    mesh_id = pl.DeviceIdType.MESH
    sides = [(axis, step) for axis in ("row", "col") for step in (1, -1)]

    def exists(axis, step):
        return me[axis] < sizes[axis] - 1 if step > 0 else me[axis] > 0

    barrier = pltpu.get_barrier_semaphore()
    for axis, step in sides:
        @pl.when(exists(axis, step))
        def _():
            pl.semaphore_signal(
                barrier, inc=1, device_id={axis: me[axis] + step}, device_id_type=mesh_id
            )
    peers = sum(jnp.where(exists(axis, step), 1, 0) for axis, step in sides)
    pl.semaphore_wait(barrier, peers)

    def push(n, src, dst, axis, step):
        copy = pltpu.make_async_remote_copy(
            src_ref=src, dst_ref=dst, send_sem=ssem.at[n], recv_sem=rsem.at[n],
            device_id={axis: me[axis] + step}, device_id_type=mesh_id,
        )

        @pl.when(exists(axis, step))
        def _():
            copy.start()

        def finish():
            @pl.when(exists(axis, step))
            def _():
                copy.wait_send()

            @pl.when(exists(axis, -step))
            def _():
                copy.wait_recv()

            @pl.when(jnp.logical_not(exists(axis, -step)))
            def _():
                dst[...] = jnp.zeros(dst.shape, dst.dtype)

        return finish

    down = push(0, mid_ref.at[pl.ds(rows - HALO, HALO)], got_top, "row", 1)
    up = push(1, mid_ref.at[pl.ds(0, HALO)], got_low, "row", -1)

    def pack(h):
        cells = row_of(mid_ref, got_top, got_low, h)
        send_left[:, h * HALO:(h + 1) * HALO] = cells[:, :HALO]
        send_right[:, h * HALO:(h + 1) * HALO] = cells[:, cols - HALO:]

    send_left[...] = jnp.zeros_like(send_left)
    send_right[...] = jnp.zeros_like(send_right)
    for h in range(HALO, HALO + rows):
        pack(h)
    down()
    up()
    for h in list(range(HALO)) + list(range(HALO + rows, tall)):
        pack(h)
    forth = push(2, send_right, got_left, "col", 1)
    back = push(3, send_left, got_right, "col", -1)
    top_ref[...] = got_top[...]
    low_ref[...] = got_low[...]
    forth()
    back()
    left_ref[...] = got_left[...]
    right_ref[...] = got_right[...]


def halos(field):
    rows, depth, cols = field.shape
    sizes = {axis: lax.axis_size(axis) for axis in ("row", "col")}
    lanes = -(-(rows + 2 * HALO) * HALO // 128) * 128
    band, strip = (HALO, depth, cols), (depth, lanes)
    return pl.pallas_call(
        functools.partial(halo_kernel, sizes),
        out_shape=[jax.ShapeDtypeStruct(v, BF16) for v in (band, band, strip, strip)],
        in_specs=[pl.BlockSpec(memory_space=pltpu.VMEM)],
        out_specs=[pl.BlockSpec(memory_space=pltpu.VMEM)] * 4,
        scratch_shapes=[pltpu.VMEM(v, BF16) for v in (band, band, strip, strip, strip, strip)]
        + [pltpu.SemaphoreType.DMA((4,)), pltpu.SemaphoreType.DMA((4,))],
        compiler_params=pltpu.CompilerParams(
            collective_id=1, has_side_effects=True, vmem_limit_bytes=16 * 1024 * 1024
        ),
        name="halos",
    )(field)


def dot(a, b):
    return jnp.dot(a, b, preferred_element_type=F32)


def dot_t(a, b):
    return lax.dot_general(a, b, (((1,), (1,)), ((), ())), preferred_element_type=F32)


def tile_kernel(
    pitch, geo, heads_in,
    mid_ref, top_ref, low_ref, left_ref, right_ref, own_ref, spread_ref, wr_ref, ws_ref, wsb_ref, we_ref, wet_ref, wc_ref, wcb_ref,
    pack_ref, stat_ref,
    x_ref, first, second, block, dlog, dsec, big, small, acc_c, reduce_ref, spatial_ref, expand_ref,
):
    chans = we_ref.shape[0]
    mid = we_ref.shape[1]
    outs = wc_ref.shape[0]
    length = x_ref.shape[1]
    shifts = [(dy - 1) * pitch + (dx - 1) for dy in range(3) for dx in range(3)]

    def columns(ref, base, sign, dest):
        rows = ref.shape[0]
        window = ref[:, pl.ds(base, STEP + 2 * EDGE)]
        for tap, shift in enumerate(shifts):
            at = EDGE + sign * shift
            dest[tap * rows:(tap + 1) * rows, :] = window[:, at:at + STEP]

    def at(i, start):
        return pl.multiple_of(start + i * STEP, 128)

    def loop(start, steps, body, init=0):
        return lax.fori_loop(0, steps, lambda i, c: body(at(i, start), c), init)

    rows, _, cols = mid_ref.shape
    tall = rows + 2 * HALO
    x_ref[:, tall * pitch // 128 * 128:] = jnp.zeros(
        (x_ref.shape[0], length - tall * pitch // 128 * 128), BF16
    )
    for h in range(tall):
        x_ref[:, h * pitch:h * pitch + HALO] = left_ref[:, h * HALO:(h + 1) * HALO]
        x_ref[:, h * pitch + HALO:h * pitch + HALO + cols] = row_of(
            mid_ref, top_ref, low_ref, h
        )
        x_ref[:, h * pitch + HALO + cols:(h + 1) * pitch] = right_ref[:, h * HALO:(h + 1) * HALO]

    first[:, :EDGE] = jnp.zeros((mid, EDGE), BF16)
    first[:, EDGE + length:] = jnp.zeros((mid, EDGE), BF16)
    dlog[...] = jnp.zeros_like(dlog)
    acc_c[...] = jnp.zeros_like(acc_c)
    reduce_ref[...] = jnp.zeros_like(reduce_ref)
    spatial_ref[...] = jnp.zeros_like(spatial_ref)
    expand_ref[...] = jnp.zeros_like(expand_ref)

    def make_first(p, c):
        z = dot(wr_ref[...], x_ref[:chans, pl.ds(p, STEP)])
        first[:, pl.ds(pl.multiple_of(p + EDGE, 128), STEP)] = jnp.maximum(z, 0.0).astype(BF16)
        return c

    loop(0, length // STEP, make_first)

    def make_block(p, c):
        columns(first, p, 1, small)
        s = jnp.maximum(dot(ws_ref[...], small[...]), 0.0).astype(BF16)
        second[:, pl.ds(p, STEP)] = s
        xs = x_ref[:, pl.ds(p, STEP)]
        valid = xs[chans + A:chans + A + 1].astype(F32)
        b = jnp.maximum(xs[:chans].astype(F32) + dot(we_ref[...], s), 0.0) * valid
        block[:, pl.ds(p, STEP)] = b.astype(BF16)
        return c

    loop(0, length // STEP, make_block)

    ident = lax.rem(lax.broadcasted_iota(jnp.int32, (outs, 1), 0), K) + 1

    def make_dlog(p, carry):
        total, count = carry
        columns(block, pl.multiple_of(p - EDGE, 128), 1, big)
        z = dot(wc_ref[...], big[...])
        code = x_ref[chans:, pl.ds(p, STEP)]
        own = own_ref[:, pl.ds(p, STEP)]
        wide = dot(spread_ref[...], code)
        live = wide >= 15.5
        label = jnp.where(live, wide - 16.0, wide)
        target = label == ident.astype(F32)
        alpha = jnp.where(target, 0.25, 0.75)
        alpha = jnp.where(live, alpha, 0.0)
        u = jnp.where(target, -z, z)
        e = jnp.exp(-jnp.abs(u))
        inv = 1.0 / (1.0 + e)
        low = e * inv
        pos = u >= 0.0
        prob = jnp.where(pos, inv, low)
        rest = jnp.where(pos, low, inv)
        soft = jnp.maximum(u, 0.0) + jnp.log1p(e)
        scaled = alpha * prob * prob
        total = total + jnp.sum(scaled * soft, axis=0, keepdims=True) * own
        slope = scaled * (2.0 * rest * soft + prob)
        d = jnp.where(target, -slope, slope).astype(BF16)
        dlog[:, pl.ds(p, STEP)] = d
        mine = (d.astype(F32) * own).astype(BF16)
        acc_c[...] += dot_t(mine, big[...])
        codes = code.astype(F32)
        labels = jnp.where(codes >= 15.5, codes - 16.0, codes)
        row = lax.broadcasted_iota(jnp.int32, codes.shape, 0)
        hit = jnp.where((labels > 0.5) & (row < A), 1.0, 0.0)
        count = count + jnp.sum(hit, axis=0, keepdims=True) * own
        return total, count

    zero = jnp.zeros((1, STEP), F32)
    total, count = loop(geo[0][0], geo[0][1], make_dlog, (zero, zero))
    stat_ref[0:1, :] = sum(total[:, k * 128:(k + 1) * 128] for k in range(STEP // 128))
    stat_ref[1:2, :] = sum(count[:, k * 128:(k + 1) * 128] for k in range(STEP // 128))
    stat_ref[2:, :] = jnp.zeros((6, 128), F32)

    def make_dsec(p, c):
        columns(dlog, pl.multiple_of(p - EDGE, 128), -1, big.at[:9 * outs])
        g = dot(wcb_ref[...], big[:9 * outs, :])
        b = block[:, pl.ds(p, STEP)].astype(F32)
        ds = jnp.where(b > 0.0, g, 0.0).astype(BF16)
        s = second[:, pl.ds(p, STEP)]
        own = own_ref[:, pl.ds(p, STEP)]
        sf = s.astype(F32)
        expand_ref[...] += dot_t((sf * own).astype(BF16), ds)
        h = dot(wet_ref[...], ds)
        dsec[:, pl.ds(p, STEP)] = jnp.where(sf > 0.0, h, 0.0).astype(BF16)
        return c

    loop(geo[0][0], geo[0][1], make_dsec)

    def make_dfirst(p, c):
        own = own_ref[:, pl.ds(p, STEP)]
        columns(first, p, 1, small)
        mine = (dsec[:, pl.ds(p, STEP)].astype(F32) * own).astype(BF16)
        spatial_ref[...] += dot_t(mine, small[...])
        columns(dsec, pl.multiple_of(p - EDGE, 128), -1, small)
        g = dot(wsb_ref[...], small[...]) * own
        f = first[:, pl.ds(pl.multiple_of(p + EDGE, 128), STEP)].astype(F32)
        df = jnp.where(f > 0.0, g, 0.0).astype(BF16)
        reduce_ref[...] += dot_t(df, x_ref[:chans, pl.ds(p, STEP)])
        return c

    loop(geo[1][0], geo[1][1], make_dfirst)
    heads = heads_in
    spots = layout(mid, heads)[:3]
    pack_ref[...] = jnp.zeros_like(pack_ref)
    for tap in range(9):
        pack_ref[tap * heads:(tap + 1) * heads, :] = acc_c[:heads, tap * chans:(tap + 1) * chans]
    pack_ref[spots[0]:spots[0] + mid, :] = reduce_ref[...]
    pack_ref[spots[1]:spots[1] + mid, :] = expand_ref[...]
    for dy in range(3):
        at_row = spots[2] + dy * mid
        pack_ref[at_row:at_row + mid, :3 * mid] = spatial_ref[:, dy * 3 * mid:(dy + 1) * 3 * mid]


def layout(mid, heads):
    first = -(-9 * heads // 8) * 8
    return first, first + mid, first + 2 * mid, first + 5 * mid


def piece_rows(s, orders, sizes, total):
    rows, out = total // len(orders), []
    for axis in orders[s]:
        rows //= sizes[axis]
        out.append(rows)
    return out


def sum_kernel(sizes, orders, pack_ref, stat_ref, out_ref, total_ref, *scratch):
    subs, depth = len(orders), len(AXES)
    send, full = scratch[0], scratch[1]
    recvs = [scratch[2 + s * depth:2 + (s + 1) * depth] for s in range(subs)]
    stat_send = scratch[2 + subs * depth]
    stat_recv = scratch[3 + subs * depth:3 + subs * depth + depth]
    ssem, rsem = scratch[-2:]
    total = pack_ref.shape[0]
    share = total // subs
    me = {axis: lax.axis_index(axis) for axis in AXES}
    peers = lambda axis: range(1, sizes[axis])
    mesh_id = pl.DeviceIdType.MESH

    barrier = pltpu.get_barrier_semaphore()
    for axis in AXES:
        for d in peers(axis):
            pl.semaphore_signal(
                barrier, inc=1, device_id={axis: lax.rem(me[axis] + d, sizes[axis])},
                device_id_type=mesh_id,
            )
    pl.semaphore_wait(barrier, sum(sizes[axis] - 1 for axis in AXES))

    used = [0]

    def push(src, dst, axis, d):
        n = used[0]
        used[0] += 1
        copy = pltpu.make_async_remote_copy(
            src_ref=src, dst_ref=dst, send_sem=ssem.at[n], recv_sem=rsem.at[n],
            device_id={axis: lax.rem(me[axis] + d, sizes[axis])}, device_id_type=mesh_id,
        )
        copy.start()
        return copy

    send[...] = pack_ref[...].astype(BF16)
    base = [s * share for s in range(subs)]
    held = [None] * subs
    stat = stat_ref[...]
    for k in range(depth):
        copies = []
        for s in range(subs):
            axis = orders[s][k]
            rows = piece_rows(s, orders, sizes, total)[k]
            for d in peers(axis):
                to = lax.rem(me[axis] + d, sizes[axis])
                src = send.at[pl.ds(pl.multiple_of(base[s] + to * rows, 16), rows)]
                copies.append(push(src, recvs[s][k].at[d - 1], axis, d))
        stat_send[k] = stat
        for d in peers(AXES[k]):
            copies.append(push(stat_send.at[k], stat_recv[k].at[d - 1], AXES[k], d))
        for copy in copies:
            copy.wait()
        for d in peers(AXES[k]):
            stat = stat + stat_recv[k][d - 1]
        for s in range(subs):
            axis = orders[s][k]
            rows = piece_rows(s, orders, sizes, total)[k]
            mine = me[axis] * rows
            if k == 0:
                got = pack_ref[pl.ds(pl.multiple_of(base[s] + mine, 16), rows), :]
            else:
                out_at = pl.ds(pl.multiple_of(base[s] + mine, 16), rows)
                got = out_ref[out_at, :]
            for d in peers(axis):
                got = got + recvs[s][k][d - 1].astype(F32)
            base[s] = pl.multiple_of(base[s] + mine, 16)
            where = pl.ds(base[s], rows)
            if k < depth - 1:
                out_ref[where, :] = got
                send[where, :] = got.astype(BF16)
            else:
                full[where, :] = got.astype(BF16)
    total_ref[...] = stat
    for k in range(depth - 1, -1, -1):
        copies = []
        for s in range(subs):
            axis = orders[s][k]
            rows = piece_rows(s, orders, sizes, total)[k]
            where = pl.ds(base[s], rows)
            for d in peers(axis):
                copies.append(push(full.at[where], full.at[where], axis, d))
            base[s] = pl.multiple_of(base[s] - me[axis] * rows, 16)
        for copy in copies:
            copy.wait()
    out_ref[...] = full[...].astype(F32)


def sum_devices(pack, stat):
    sizes = {axis: lax.axis_size(axis) for axis in AXES}
    orders = [AXES[s:] + AXES[:s] for s in range(len(AXES))]
    total, chans = pack.shape
    scratch = [pltpu.VMEM((total, chans), BF16), pltpu.VMEM((total, chans), BF16)]
    copies = 0
    for s in range(len(orders)):
        for axis, rows in zip(orders[s], piece_rows(s, orders, sizes, total)):
            scratch.append(pltpu.VMEM((max(sizes[axis] - 1, 1), rows, chans), BF16))
            copies += 2 * (sizes[axis] - 1)
    scratch.append(pltpu.VMEM((len(AXES),) + stat.shape, F32))
    for axis in AXES:
        scratch.append(pltpu.VMEM((max(sizes[axis] - 1, 1),) + stat.shape, F32))
        copies += sizes[axis] - 1
    scratch += [pltpu.SemaphoreType.DMA((copies,)), pltpu.SemaphoreType.DMA((copies,))]
    return pl.pallas_call(
        functools.partial(sum_kernel, sizes, orders),
        out_shape=(
            jax.ShapeDtypeStruct(pack.shape, F32), jax.ShapeDtypeStruct(stat.shape, F32)
        ),
        in_specs=[pl.BlockSpec(memory_space=pltpu.VMEM)] * 2,
        out_specs=[pl.BlockSpec(memory_space=pltpu.VMEM)] * 2,
        scratch_shapes=scratch,
        compiler_params=pltpu.CompilerParams(
            collective_id=0, has_side_effects=True, vmem_limit_bytes=16 * 1024 * 1024
        ),
        name="sum_devices",
    )(pack, stat)


def per_device(
    inputs, reduce_weight, spatial_weight, expand_weight, class_weight, anchor_labels, anchor_mask
):
    tiles, chans, rows, cols = inputs.shape
    mid = reduce_weight.shape[0]
    heads = class_weight.shape[2]
    outs = -(-heads // 16) * 16
    tall, pitch = rows + 2 * HALO, cols + 2 * HALO
    pixels = tall * pitch
    length = -(-pixels // STEP) * STEP

    def span(margin):
        low = margin * pitch + margin
        high = (tall - margin) * pitch
        start = max(EDGE, low // 128 * 128 // EDGE * EDGE)
        return start, -(-(high - start) // STEP)

    geo = (span(2), span(4))
    need = geo[0][0] + geo[0][1] * STEP + EDGE
    length = max(length, -(-need // STEP) * STEP)

    code = (anchor_labels + 16 * anchor_mask).astype(BF16)
    ones = jnp.ones((tiles, 1, rows, cols), BF16)
    none = jnp.zeros((tiles, 16 - A - 1, rows, cols), BF16)
    field = jnp.concatenate([inputs, code, ones, none], axis=1)
    field = field.transpose(0, 2, 1, 3)

    own = np.zeros((tall, pitch), np.float32)
    own[HALO:HALO + rows, HALO:HALO + cols] = 1.0
    own = jnp.asarray(np.pad(own.reshape(1, pixels), ((0, 0), (0, length - pixels))))
    spread = np.zeros((outs, 16), np.float32)
    spread[np.arange(heads), np.arange(heads) // K] = 1.0
    spread = jnp.asarray(spread, BF16)

    ws = spatial_weight.transpose(2, 0, 1, 3).reshape(mid, 9 * mid)
    wsb = spatial_weight.transpose(3, 0, 1, 2).reshape(mid, 9 * mid)
    wide = jnp.pad(class_weight, ((0, 0), (0, 0), (0, outs - heads), (0, 0)))
    wc = wide.transpose(2, 0, 1, 3).reshape(outs, 9 * chans)
    wcb = wide.transpose(3, 0, 1, 2).reshape(chans, 9 * outs)

    unit = 16 * len(AXES) * int(np.prod([lax.axis_size(axis) for axis in AXES]))
    packed = -(-layout(mid, heads)[3] // unit) * unit

    call = pl.pallas_call(
        functools.partial(tile_kernel, pitch, geo, heads),
        out_shape=(
            jax.ShapeDtypeStruct((packed, chans), F32),
            jax.ShapeDtypeStruct((8, 128), F32),
        ),
        in_specs=[pl.BlockSpec(memory_space=pltpu.VMEM)] * 14,
        out_specs=[pl.BlockSpec(memory_space=pltpu.VMEM)] * 2,
        scratch_shapes=[
            pltpu.VMEM((chans + 16, length), BF16),
            pltpu.VMEM((mid, length + 2 * EDGE), BF16),
            pltpu.VMEM((mid, length), BF16),
            pltpu.VMEM((chans, length), BF16),
            pltpu.VMEM((outs, length), BF16),
            pltpu.VMEM((mid, length), BF16),
            pltpu.VMEM((9 * chans, STEP), BF16),
            pltpu.VMEM((9 * mid, STEP), BF16),
            pltpu.VMEM((outs, 9 * chans), F32),
            pltpu.VMEM((mid, chans), F32),
            pltpu.VMEM((mid, 9 * mid), F32),
            pltpu.VMEM((mid, chans), F32),
        ],
        compiler_params=pltpu.CompilerParams(vmem_limit_bytes=50 * 1024 * 1024),
        name="tile_step",
    )
    sums = None
    for t in range(tiles):
        part = call(
            field[t], *halos(field[t]), own, spread, reduce_weight, ws, wsb, expand_weight, expand_weight.T, wc, wcb
        )
        sums = part if sums is None else tuple(a + b for a, b in zip(sums, part))
    return finish(sums, mid, heads)


def finish(sums, mid, heads):
    pack, stat = sum_devices(*sums)
    chans = pack.shape[1]
    spots = layout(mid, heads)
    count = jnp.sum(stat[1])
    scale = 1.0 / count
    spatial = pack[spots[2]:spots[3], :3 * mid].reshape(3, mid, 3, mid).transpose(0, 2, 1, 3)
    return (
        jnp.sum(stat[0]) / count,
        pack[spots[0]:spots[1]] * scale,
        spatial * scale,
        pack[spots[1]:spots[2]].T * scale,
        pack[:9 * heads].reshape(3, 3, heads, chans) * scale,
    )


def solution(mesh):
    tiled = P("dp", None, "row", "col")
    return jax.shard_map(
        per_device,
        mesh=mesh,
        in_specs=(tiled, P(), P(), P(), P(), tiled, tiled),
        out_specs=(P(), P(), P(), P(), P()),
        check_vma=False,
    )
```
